1024 devices in a mesh: fsdp: 256 (over x, z_lo, y, core), ctx: 4 (over z_hi).
Axes of the slice: x: 4, y: 8, z: 16 (z_hi: 4, z_lo: 4; z = z_hi * 4 + z_lo), core: 2. Of those that a mesh axis runs over, the one named last changes fastest.
Arguments:
- hidden_states: bfloat16 [256, 1536, 4096], P('fsdp', 'ctx'), may hold values from -20.4 to 20.4
- qkv_weight: bfloat16 [4096, 768], P('fsdp'), may hold values from -0.09375 to 0.09375
- doc_ids: int32 [256, 1536], P('fsdp', 'ctx'), may hold values from 0 to 1, never falling along the last dimension, each value on 1 to 1344 neighbouring positions
Outputs:
- context: bfloat16 [256, 1536, 512], P('fsdp', 'ctx')
The draws below stay inside these ranges and needn't reach their ends.
Inputs may be any that keep to these rules, and one draw needn't show every extreme that they name: `doc_ids`: each sequence holds two documents one after the other, numbered 0 then 1, never falling; the first has 192 to 1344 tokens and the second the rest.
All inputs are finite; a program needn't handle non-finite values.
Results may differ from the reference program's by a relative error of at most 0.012.
The reference program's roundings to bfloat16 on the way (of `queries`, `keys`, `values` and `probs`) count: a program that leaves them out, or rounds other values in their place, can miss the bound.
Values may be sent and summed in bfloat16 or wider, within the bound.
A program may use at most 32 MiB of HBM per device.

```python
import math
import jax
import jax.numpy as jnp
import numpy as np
from jax import lax

D = 4096
HEADS = 4
HD = 128
TOK_DEV = 384
SEQ = 1536
SEQS = 256
COLS = 768


def draw_hidden_states(key, part):
    key_one = jax.random.fold_in(jax.random.fold_in(key, 11), 0)
    bulk_values = jax.random.normal(key_one, (SEQS, SEQ, D), jnp.float32)
    return jnp.clip(bulk_values, -6.0, 6.0).astype(jnp.bfloat16)


def levels(key, shape, cuts, low, high):
    factor_of = 1.0
    for dim, parts in cuts:
        draws = jax.random.uniform(jax.random.fold_in(jax.random.fold_in(key, 6), dim), (parts,), jnp.float32, low / len(cuts), high / len(cuts))
        factor_of = factor_of * jnp.repeat(jnp.exp(draws), shape[dim] // parts).reshape((-1,) + (1,) * (len(shape) - 1 - dim))
    return factor_of


def length_profile(amount, total, limit, lean):
    weights = [(1 << 20) // math.isqrt(rank ** lean) + 1 for rank in range(2, amount + 1)]
    spare, given = total - limit - (amount - 1), [1] * (amount - 1)
    while spare > 0:
        free = [i for i in range(amount - 1) if given[i] < limit]
        pool, remaining = sum([weights[i] for i in free]), spare
        for i in free:
            extra = min(limit - given[i], max(1, remaining * weights[i] // pool), spare)
            given[i] = given[i] + extra
            spare = spare - extra
    return np.array([limit] + given)


def uneven_parts(rng, number_of, total, limit, slope):
    if number_of == 2:
        one = jax.random.randint(rng, (), max(1, total - limit), min(limit, total - 1) + 1)
        return jnp.stack([one, total - one])
    sizes = jnp.asarray(length_profile(number_of, total, limit, slope), jnp.int32)
    pairs = (number_of - 1) // 2
    giver, receiver = sizes[1:1 + 2 * pairs:2], sizes[2:2 + 2 * pairs:2]
    room = jnp.minimum(giver - 1, limit - receiver)
    shifted = jax.random.randint(jax.random.fold_in(rng, 1), (pairs,), 0, 1 << 20) % (room + 1)
    sizes = sizes.at[1:1 + 2 * pairs:2].set(giver - shifted).at[2:2 + 2 * pairs:2].set(receiver + shifted)
    return sizes[jax.random.permutation(jax.random.fold_in(rng, 2), number_of)]


def gaussian(rng, dims, scale, limit, cuts=(), held_as=jnp.bfloat16):
    loudness = levels(rng, dims, cuts, -0.22, 0.18) if cuts else 1.0
    array = jax.random.normal(rng, dims, jnp.float32) * scale * loudness
    return jnp.minimum(jnp.maximum(array, -limit), limit).astype(held_as)


def setup_inputs(seed: int = 0) -> dict:
    arg_keys = jax.random.split(jax.random.key(seed), 4)
    hidden_states = draw_hidden_states(jax.random.fold_in(arg_keys[3], 71), 0)
    qkv_weight = gaussian(arg_keys[1], (D, COLS), D ** -0.5, 0.09375, ((0, 256),))
    doc_ids = jax.vmap(lambda own: jnp.searchsorted(jnp.cumsum(uneven_parts(own, 2, SEQ, SEQ - TOK_DEV // 2, 0)), jnp.arange(SEQ), side="right"))(jax.random.split(arg_keys[2], SEQS)).reshape((SEQS, SEQ)).astype(jnp.int32)
    return dict(hidden_states=hidden_states, qkv_weight=qkv_weight, doc_ids=doc_ids)


THETA = 1000000.0

def rotary(values_in, positions):
    half_width = values_in.shape[-1] // 2
    frequency = jnp.exp(jnp.arange(half_width, dtype=jnp.float32) * (-2.0 * math.log(THETA) / values_in.shape[-1]))
    angles = positions * frequency
    cosine = jnp.cos(angles)
    sine_part = jnp.sin(angles)
    lower_half = values_in[..., :half_width]
    upper_half = values_in[..., half_width:]
    return jnp.concatenate([lower_half * cosine - upper_half * sine_part, upper_half * cosine + lower_half * sine_part], axis=-1)

def reference(hidden_states, qkv_weight, doc_ids):
    scale = 1.0 / math.sqrt(HD)

    def one_sequence(inputs):
        tokens, documents = inputs
        length = tokens.shape[0]
        projected = jnp.dot(tokens, qkv_weight, preferred_element_type=jnp.float32)
        positions = jnp.arange(length, dtype=jnp.int32).astype(jnp.float32)
        queries = rotary(projected[:, :HEADS * HD].reshape(length, HEADS, HD), positions[:, None, None]).astype(jnp.bfloat16)
        keys = rotary(projected[:, HEADS * HD:(HEADS + 1) * HD], positions[:, None]).astype(jnp.bfloat16)
        values = projected[:, (HEADS + 1) * HD:].astype(jnp.bfloat16)
        scores = jnp.einsum('qhd,kd->hqk', queries.astype(jnp.float32), keys.astype(jnp.float32)) * scale
        index = jnp.arange(length, dtype=jnp.int32)
        visible = (index[None, :] <= index[:, None]) & (documents[None, :] == documents[:, None])
        scores = jnp.where(visible[None], scores, -jnp.inf)
        row_max = lax.optimization_barrier(jnp.max(scores, axis=-1, keepdims=True))
        weights = jnp.exp(scores - row_max)
        totals = lax.optimization_barrier(jnp.sum(weights, axis=-1))
        probs = weights.astype(jnp.bfloat16)
        summed = jnp.einsum('hqk,kd->hqd', probs.astype(jnp.float32), values.astype(jnp.float32))
        context = (summed / totals[..., None]).astype(jnp.bfloat16)
        return jnp.transpose(context, (1, 0, 2)).reshape(length, HEADS * HD)
    return lax.map(one_sequence, (hidden_states, doc_ids))
```

```python
import functools
import math

import jax
import jax.numpy as jnp
from jax import lax
from jax.experimental import pallas as pl
from jax.experimental.pallas import tpu as pltpu
from jax.sharding import PartitionSpec as P

MESH = pl.DeviceIdType.MESH
HEADS = 4
HD = 128
THETA = 1000000.0
X, ZL, Y, ZH = 4, 4, 8, 4
Z = ZL * ZH
SCALE2 = math.log2(math.e) / math.sqrt(HD)


def kernel(hid, w_in, doc, out, wbuf, hbuf, kv, docs, qs, acc, m_s, l_s, bias, cos_s, sin_s,
           loc_sem, zs, zr, rs, rr, ss, sr, kvs, kvr, ds, dr):
    rows = hid.shape[1]
    shard = w_in.shape[0]
    depth = X * ZL * Y * 2 * shard
    f = lax.axis_index("fsdp")
    ctx = lax.axis_index("ctx")
    core = lax.rem(f, 2)
    y = lax.rem(f // 2, Y)
    zl = lax.rem(f // (2 * Y), ZL)
    x = f // (2 * Y * ZL)
    z = ctx * ZL + zl

    def device(x_, z_, y_, core_):
        return {"fsdp": ((x_ * ZL + lax.rem(z_, ZL)) * Y + y_) * 2 + core_, "ctx": z_ // ZL}

    def shift(v, d, n):
        return lax.rem(v + d + n, n)

    z_peers = [shift(z, 1, Z), shift(z, -1, Z), shift(z, 2, Z)]
    sibling = device(x, z, y, 1 - core)
    x_right, x_left = device(shift(x, 1, X), z, y, core), device(shift(x, -1, X), z, y, core)
    y_right, y_left = device(x, z, shift(y, 1, Y), core), device(x, z, shift(y, -1, Y), core)
    ctx_right = {"fsdp": f, "ctx": shift(ctx, 1, ZH)}
    ctx_left = {"fsdp": f, "ctx": shift(ctx, -1, ZH)}

    def remote(src, dst, send, recv, dev):
        return pltpu.make_async_remote_copy(
            src_ref=src, dst_ref=dst, send_sem=send, recv_sem=recv, device_id=dev,
            device_id_type=MESH,
        )

    barrier = pltpu.get_barrier_semaphore()
    peers = [sibling, x_right, x_left, y_right, y_left, ctx_right, ctx_left]
    for z_ in z_peers + [shift(z, -2, Z)]:
        peers += [device(x, z_, y, 0), device(x, z_, y, 1)]
    hid_copy = pltpu.make_async_copy(hid.at[0], hbuf, loc_sem.at[0])
    hid_copy.start()
    for dev in peers:
        pl.semaphore_signal(barrier, inc=1, device_id=dev, device_id_type=MESH)
    pl.semaphore_wait(barrier, len(peers))

    def column(j, cc):
        start = (HEADS + cc) * HD if j == 0 else ((j - 1) * 2 + cc) * HD
        return pl.ds(pl.multiple_of(start, HD), HD)

    def z_slot(j, cc, zl_, core_):
        return wbuf.at[j, cc, x, zl_, y, pl.ds(pl.multiple_of(core_ * shard, shard), shard)]

    def z_send(j, k):
        cc = 1 - core if k % 2 else core
        if k < 2:
            dev = sibling
        else:
            dev = device(x, z_peers[k // 2 - 1], y, cc)
        return remote(
            w_in.at[:, column(j, cc)], z_slot(j, cc, zl, core), zs.at[j, k], zr.at[j, k], dev
        )

    def z_own(j):
        return pltpu.make_async_copy(
            w_in.at[:, column(j, core)], z_slot(j, core, zl, core), zr.at[j, 0]
        )

    def z_wait(j):
        z_own(j).wait()
        for k in range(1, 8):
            from_core = 1 - core if k % 2 else core
            from_zl = lax.rem(zl + (0, -1, 1, -2)[k // 2] + ZL, ZL)
            slot = z_slot(j, core, from_zl, from_core)
            remote(slot, slot, zs.at[j, k], zr.at[j, k], sibling).wait_recv()

    for j in range(3):
        z_own(j).start()
        for k in (7, 6, 5, 4, 3, 2, 1):
            z_send(j, k).start()

    doc_right = remote(doc, docs.at[ctx], ds.at[0], dr.at[ctx], ctx_right)
    doc_left = remote(doc, docs.at[ctx], ds.at[1], dr.at[ctx], ctx_left)
    before = jnp.maximum(ctx - 1, 0)
    doc_relay = remote(docs.at[before], docs.at[before], ds.at[2], dr.at[before], ctx_right)

    @pl.when(ctx < ZH - 1)
    def _():
        doc_right.start()

    @pl.when(ctx == 0)
    def _():
        doc_left.start()

    lane = lax.broadcasted_iota(jnp.int32, (1, HD), 1)
    half_lane = jnp.where(lane < HD // 2, lane, lane - HD // 2).astype(jnp.float32)
    frequency = jnp.exp(half_lane * (-2.0 * math.log(THETA) / HD))
    position = (ctx * rows + lax.broadcasted_iota(jnp.int32, (rows, 1), 0)).astype(jnp.float32)
    angles = position * frequency
    cos_s[...] = jnp.cos(angles)
    sin_s[...] = jnp.sin(angles) * jnp.where(lane < HD // 2, -1.0, 1.0)

    def rotary(v):
        return (v * cos_s[...] + pltpu.roll(v, HD // 2, 1) * sin_s[...]).astype(jnp.bfloat16)

    def block(stage, cc, js, i, half=None):
        zz = slice(None) if half is None else slice(half * (ZL // 2), (half + 1) * (ZL // 2))
        along_x = (stage == 0) == (cc == 1)
        if along_x:
            if stage == 0:
                return wbuf.at[js, cc, i, zz, y]
            return wbuf.at[js, cc, i, zz]
        if stage == 0:
            return wbuf.at[js, cc, x, zz, i]
        return wbuf.at[js, cc, :, zz, i]

    class Ring:
        def __init__(self, phase, stage, cc):
            self.phase, self.stage, self.cc = phase, stage, cc
            self.js = slice(0, 1) if phase == 0 else slice(1, 3)
            along_x = (stage == 0) == (cc == 1)
            self.n = X if along_x else Y
            self.p = x if along_x else y
            self.dev = (x_right, x_left) if along_x else (y_right, y_left)
            self.steps = self.n // 2

        def received(self, d, s):
            half = d if s == self.steps else None
            return block(self.stage, self.cc, self.js,
                         shift(self.p, -s if d == 0 else s, self.n), half)

        def copy(self, d, s):
            half = d if s == self.steps else None
            i = shift(self.p, 1 - s if d == 0 else s - 1, self.n)
            ref = block(self.stage, self.cc, self.js, i, half)
            at = (self.phase, self.stage, d, s - 1)
            return remote(ref, ref, rs.at[at], rr.at[at], self.dev[d])

        def start(self, s):
            for d in range(2):
                self.copy(d, s).start()

        def wait(self, s, d):
            ref = self.received(d, s)
            at = (self.phase, self.stage, d, s - 1)
            remote(ref, ref, rs.at[at], rr.at[at], self.dev[d]).wait_recv()

        def done(self):
            for s in range(1, self.steps + 1):
                for d in range(2):
                    self.copy(d, s).wait_send()

        def pieces(self):
            own = [block(self.stage, self.cc, self.js, self.p)]
            return own + [self.received(d, s) for s in range(1, self.steps + 1) for d in range(2)]

    def forward(ring, k):
        ref = ring.pieces()[k]
        at = (ring.phase, k)
        return remote(ref, ref, ss.at[at], sr.at[at], sibling)

    def last_stage(ring):
        ring.start(1)
        forward(ring, 0).start()
        for s in range(1, ring.steps + 1):
            for d in range(2):
                ring.wait(s, d)
                if s < ring.steps:
                    ring.copy(d, s + 1).start()
            for d in range(2):
                forward(ring, 1 + (s - 1) * 2 + d).start()

    def n_pieces(ring):
        return 1 + 2 * ring.steps

    def project(j, groups):
        chunk = depth // X

        def step(i, total):
            w = jnp.concatenate(
                [wbuf[j, cc, i].reshape(chunk, HD) for cc in groups], axis=1
            ) if len(groups) > 1 else wbuf[j, groups[0], i].reshape(chunk, HD)
            h = hbuf[:, pl.ds(pl.multiple_of(i * chunk, chunk), chunk)]
            return total + jnp.dot(h, w, preferred_element_type=jnp.float32)

        return lax.fori_loop(0, X, step, jnp.zeros((rows, HD * len(groups)), jnp.float32))

    def kv_copy(kind, way):
        if way == 0:
            return remote(kv.at[kind, ctx], kv.at[kind, ctx], kvs.at[kind, 0],
                          kvr.at[kind, ctx], ctx_right)
        if way == 1:
            return remote(kv.at[kind, ctx], kv.at[kind, ctx], kvs.at[kind, 1],
                          kvr.at[kind, ctx], ctx_left)
        b = before if kind == 0 else jnp.where(ctx == 0, 1, 0)
        dev = ctx_right if kind == 0 else ctx_left
        return remote(kv.at[kind, b], kv.at[kind, b], kvs.at[kind, 2], kvr.at[kind, b], dev)

    def kv_sends(kind, act):
        left = ctx == 0 if kind == 0 else ctx <= 1

        @pl.when(left)
        def _():
            act(kv_copy(kind, 1))

        @pl.when(ctx < ZH - 1)
        def _():
            act(kv_copy(kind, 0))

    def make(kind):
        if kind == 0:
            kv[0, ctx] = rotary(project(0, (0,)))
        else:
            kv[1, ctx] = project(0, (1,)).astype(jnp.bfloat16)
        kv_sends(kind, lambda c: c.start())

    for cc in range(2):

        @pl.when(core == cc)
        def _():
            kv1, kv2, q1, q2 = Ring(0, 0, cc), Ring(0, 1, cc), Ring(1, 0, cc), Ring(1, 1, cc)
            other1, other2 = Ring(0, 1, 1 - cc), Ring(1, 1, 1 - cc)
            z_wait(0)
            kv1.start(1)
            z_wait(1)
            z_wait(2)
            q1.start(1)
            for s in range(1, kv1.steps + 1):
                for ring in (kv1, q1):
                    for d in range(2):
                        ring.wait(s, d)
                        if s < ring.steps:
                            ring.copy(d, s + 1).start()
            last_stage(kv2)
            hid_copy.wait()
            make(cc)
            for k in range(n_pieces(other1)):
                forward(other1, k).wait_recv()
            make(1 - cc)
            last_stage(q2)
            for k in range(n_pieces(other2)):
                forward(other2, k).wait_recv()
            for ring in (kv1, kv2, q1, q2):
                ring.done()
            for ring in (kv2, q2):
                for k in range(n_pieces(ring)):
                    forward(ring, k).wait_send()

    for j in range(3):
        for k in range(1, 8):
            z_send(j, k).wait_send()

    def arrived(kind, b):
        remote(kv.at[kind, b], kv.at[kind, b], kvs.at[kind, 0], kvr.at[kind, b],
               ctx_right).wait_recv()

    def docs_arrived(b):
        remote(docs.at[b], docs.at[b], ds.at[0], dr.at[b], ctx_right).wait_recv()

    @pl.when((ctx == 1) | (ctx == 2))
    def _():
        docs_arrived(before)
        doc_relay.start()
        arrived(0, before)
        kv_copy(0, 2).start()

    @pl.when((ctx == 0) | (ctx == 3))
    def _():
        arrived(1, jnp.where(ctx == 0, 1, 0))
        kv_copy(1, 2).start()

    for j in range(2):
        pair = project(1 + j, (0, 1))
        for i in range(2):
            qs[2 * j + i] = rotary(pair[:, i * HD : (i + 1) * HD])

    token = lax.broadcasted_iota(jnp.int32, (rows, 1), 0)
    zeros_here = jnp.sum(jnp.where(doc[...] == 0, 1.0, 0.0), axis=1, keepdims=True)
    doc_query = jnp.where(token.astype(jnp.float32) >= zeros_here, 1.0, 0.0)

    def scores(h, b):
        s = lax.dot_general(
            qs[h], kv[0, b], (((1,), (1,)), ((), ())), preferred_element_type=jnp.float32
        )
        return s * SCALE2 + bias[...]

    same = doc_query == doc[...].astype(jnp.float32)
    causal = lax.broadcasted_iota(jnp.int32, (rows, rows), 1) <= token
    bias[...] = jnp.where(same & causal, 0.0, -jnp.inf)

    def first(h, _):
        s = scores(h, ctx)
        top = jnp.max(s, axis=1, keepdims=True)
        p = jnp.exp2(s - top)
        m_s[h] = top
        l_s[h] = jnp.sum(p, axis=1, keepdims=True)
        acc[h] = jnp.dot(p.astype(jnp.bfloat16), kv[1, ctx], preferred_element_type=jnp.float32)
        return 0

    lax.fori_loop(0, HEADS, first, 0)

    def later(t, _):
        b = jnp.where(t == 0, ctx - 1, t - 1)

        @pl.when(jnp.logical_not(((ctx == 1) | (ctx == 2)) & (b == ctx - 1)))
        def _():
            docs_arrived(b)
            arrived(0, b)

        @pl.when(jnp.logical_not((ctx == 3) & (b == 0)))
        def _():
            arrived(1, b)

        bias[...] = jnp.where(doc_query == docs[b].astype(jnp.float32), 0.0, -jnp.inf)

        def update(h, _):
            s = scores(h, b)
            old = m_s[h]
            top = jnp.maximum(old, jnp.max(s, axis=1, keepdims=True))
            p = jnp.exp2(s - top)
            factor = jnp.exp2(old - top)
            m_s[h] = top
            l_s[h] = l_s[h] * factor + jnp.sum(p, axis=1, keepdims=True)
            acc[h] = acc[h] * factor + jnp.dot(
                p.astype(jnp.bfloat16), kv[1, b], preferred_element_type=jnp.float32
            )
            return 0

        lax.fori_loop(0, HEADS, update, 0)
        return 0

    lax.fori_loop(0, ctx, later, 0)

    for h in range(HEADS):
        out[:, h * HD : (h + 1) * HD] = (acc[h] / l_s[h]).astype(jnp.bfloat16)

    for kind in range(2):
        kv_sends(kind, lambda c: c.wait_send())

    @pl.when(ctx < ZH - 1)
    def _():
        doc_right.wait_send()

    @pl.when(ctx == 0)
    def _():
        doc_left.wait_send()

    @pl.when((ctx == 1) | (ctx == 2))
    def _():
        doc_relay.wait_send()
        kv_copy(0, 2).wait_send()

    @pl.when((ctx == 0) | (ctx == 3))
    def _():
        kv_copy(1, 2).wait_send()


def body(hidden_states, qkv_weight, doc_ids):
    rows, width = hidden_states.shape[1:]
    shard = qkv_weight.shape[0]
    dma = pltpu.SemaphoreType.DMA
    steps = max(X, Y) // 2
    result = pl.pallas_call(
        kernel,
        out_shape=jax.ShapeDtypeStruct((rows, HEADS * HD), jnp.bfloat16),
        in_specs=[
            pl.BlockSpec(memory_space=pl.ANY),
            pl.BlockSpec(memory_space=pl.ANY),
            pl.BlockSpec(memory_space=pltpu.VMEM),
        ],
        out_specs=pl.BlockSpec(memory_space=pltpu.VMEM),
        scratch_shapes=[
            pltpu.VMEM((3, 2, X, ZL, Y, 2 * shard, HD), jnp.bfloat16),
            pltpu.VMEM((rows, width), jnp.bfloat16),
            pltpu.VMEM((2, ZH, rows, HD), jnp.bfloat16),
            pltpu.VMEM((ZH, 1, rows), jnp.int32),
            pltpu.VMEM((HEADS, rows, HD), jnp.bfloat16),
            pltpu.VMEM((HEADS, rows, HD), jnp.float32),
            pltpu.VMEM((HEADS, rows, 1), jnp.float32),
            pltpu.VMEM((HEADS, rows, 1), jnp.float32),
            pltpu.VMEM((rows, rows), jnp.float32),
            pltpu.VMEM((rows, HD), jnp.float32),
            pltpu.VMEM((rows, HD), jnp.float32),
            dma((1,)),
            dma((3, 8)),
            dma((3, 8)),
            dma((2, 2, 2, steps)),
            dma((2, 2, 2, steps)),
            dma((2, 2 * steps + 1)),
            dma((2, 2 * steps + 1)),
            dma((2, 3)),
            dma((2, ZH)),
            dma((3,)),
            dma((ZH,)),
        ],
        compiler_params=pltpu.CompilerParams(
            collective_id=0, has_side_effects=True, vmem_limit_bytes=60 * 1024 * 1024
        ),
    )(hidden_states, qkv_weight, doc_ids)
    return result[None]


def solution(mesh):
    in_specs = (P("fsdp", "ctx", None), P("fsdp", None), P("fsdp", "ctx"))
    out_specs = P("fsdp", "ctx", None)
    return jax.shard_map(body, mesh=mesh, in_specs=in_specs, out_specs=out_specs, check_vma=False)
```

```python
import functools
import math

import jax
import jax.numpy as jnp
from jax import lax
from jax.experimental import pallas as pl
from jax.experimental.pallas import tpu as pltpu
from jax.sharding import PartitionSpec as P

MESH = pl.DeviceIdType.MESH
HEADS = 4
HD = 128
THETA = 1000000.0
X, ZL, Y, ZH = 4, 4, 8, 4
Z = ZL * ZH
SCALE2 = math.log2(math.e) / math.sqrt(HD)


def kernel(hid, w_in, doc, out, wbuf, hbuf, kv, docs, qs, acc, m_s, l_s, bias, cos_s, sin_s,
           loc_sem, zs, zr, s1, r1, s2, r2, ss, sr, kvs, kvr, ds, dr):
    rows = hid.shape[1]
    shard = w_in.shape[0]
    depth = X * ZL * Y * 2 * shard
    f = lax.axis_index("fsdp")
    ctx = lax.axis_index("ctx")
    core = lax.rem(f, 2)
    y = lax.rem(f // 2, Y)
    zl = lax.rem(f // (2 * Y), ZL)
    x = f // (2 * Y * ZL)
    z = ctx * ZL + zl

    def device(x_, z_, y_, core_):
        return {"fsdp": ((x_ * ZL + lax.rem(z_, ZL)) * Y + y_) * 2 + core_, "ctx": z_ // ZL}

    def shift(v, d, n):
        return lax.rem(v + d + n, n)

    z_peers = [shift(z, 1, Z), shift(z, -1, Z), shift(z, 2, Z)]
    sibling = device(x, z, y, 1 - core)
    x_right, x_left = device(shift(x, 1, X), z, y, core), device(shift(x, -1, X), z, y, core)
    y_right, y_left = device(x, z, shift(y, 1, Y), core), device(x, z, shift(y, -1, Y), core)
    ctx_right = {"fsdp": f, "ctx": shift(ctx, 1, ZH)}
    ctx_left = {"fsdp": f, "ctx": shift(ctx, -1, ZH)}

    def remote(src, dst, send, recv, dev):
        return pltpu.make_async_remote_copy(
            src_ref=src, dst_ref=dst, send_sem=send, recv_sem=recv, device_id=dev,
            device_id_type=MESH,
        )

    barrier = pltpu.get_barrier_semaphore()
    peers = [ctx_right, ctx_left, sibling]
    peers += [device(shift(x, d, X), z, y, core) for d in range(1, X)]
    peers += [device(x, z, shift(y, d, Y), core) for d in range(1, Y)]
    for z_ in z_peers + [shift(z, -2, Z)]:
        peers += [device(x, z_, y, 0), device(x, z_, y, 1)]
    hid_copy = pltpu.make_async_copy(hid.at[0], hbuf, loc_sem.at[0])
    hid_copy.start()
    for dev in peers:
        pl.semaphore_signal(barrier, inc=1, device_id=dev, device_id_type=MESH)
    pl.semaphore_wait(barrier, len(peers))

    def column(j, cc):
        start = (HEADS + cc) * HD if j == 0 else ((j - 1) * 2 + cc) * HD
        return pl.ds(pl.multiple_of(start, HD), HD)

    def z_slot(j, cc, zl_, core_):
        return wbuf.at[j, cc, x, zl_, y, pl.ds(pl.multiple_of(core_ * shard, shard), shard)]

    def z_send(j, k):
        cc = 1 - core if k % 2 else core
        if k < 2:
            dev = sibling
        else:
            dev = device(x, z_peers[k // 2 - 1], y, cc)
        return remote(
            w_in.at[:, column(j, cc)], z_slot(j, cc, zl, core), zs.at[j, k], zr.at[j, k], dev
        )

    def z_own(j):
        return pltpu.make_async_copy(
            w_in.at[:, column(j, core)], z_slot(j, core, zl, core), zr.at[j, 0]
        )

    def z_wait(j):
        z_own(j).wait()
        for k in range(1, 8):
            from_core = 1 - core if k % 2 else core
            from_zl = lax.rem(zl + (0, -1, 1, -2)[k // 2] + ZL, ZL)
            slot = z_slot(j, core, from_zl, from_core)
            remote(slot, slot, zs.at[j, k], zr.at[j, k], sibling).wait_recv()

    for j in range(3):
        z_own(j).start()
        for k in (7, 6, 5, 4, 3, 2, 1):
            z_send(j, k).start()

    doc_right = remote(doc, docs.at[ctx], ds.at[0], dr.at[ctx], ctx_right)
    doc_left = remote(doc, docs.at[ctx], ds.at[1], dr.at[ctx], ctx_left)
    before = jnp.maximum(ctx - 1, 0)
    doc_relay = remote(docs.at[before], docs.at[before], ds.at[2], dr.at[before], ctx_right)

    @pl.when(ctx < ZH - 1)
    def _():
        doc_right.start()

    @pl.when(ctx == 0)
    def _():
        doc_left.start()

    lane = lax.broadcasted_iota(jnp.int32, (1, HD), 1)
    half_lane = jnp.where(lane < HD // 2, lane, lane - HD // 2).astype(jnp.float32)
    frequency = jnp.exp(half_lane * (-2.0 * math.log(THETA) / HD))
    position = (ctx * rows + lax.broadcasted_iota(jnp.int32, (rows, 1), 0)).astype(jnp.float32)
    angles = position * frequency
    cos_s[...] = jnp.cos(angles)
    sin_s[...] = jnp.sin(angles) * jnp.where(lane < HD // 2, -1.0, 1.0)

    def rotary(v):
        return (v * cos_s[...] + pltpu.roll(v, HD // 2, 1) * sin_s[...]).astype(jnp.bfloat16)

    class Gather:
        def __init__(self, phase, cc):
            self.phase, self.cc = phase, cc
            self.js = slice(0, 1) if phase == 0 else slice(1, 3)
            self.n1, self.p1 = (Y, y) if cc == 0 else (X, x)
            self.n2, self.p2 = (X, x) if cc == 0 else (Y, y)
            self.dev = (x_right, x_left) if cc == 0 else (y_right, y_left)
            self.steps = self.n2 // 2

        def piece(self, i, q, half=None):
            zz = slice(None) if half is None else slice(half * (ZL // 2), (half + 1) * (ZL // 2))
            if self.cc == 0:
                return wbuf.at[self.js, 0, q, zz, i]
            return wbuf.at[self.js, 1, i, zz, q]

        def offset(self, k):
            return (k + 1) // 2 * (1 - 2 * lax.rem(k + 1, 2))

        def direct(self, k):
            ref = self.piece(self.p1, self.p2)
            to = lax.rem(self.p1 + self.offset(k) + self.n1, self.n1)
            dev = device(x, z, to, core) if self.cc == 0 else device(to, z, y, core)
            return remote(ref, ref, s1.at[self.phase, k], r1.at[self.phase, k], dev)

        def index(self, k):
            return lax.rem(self.p1 - self.offset(k) + self.n1, self.n1)

        def at(self, d, s, k):
            half = d if s == self.steps else None
            return self.piece(self.index(k), shift(self.p2, -s if d == 0 else s, self.n2), half)

        def copy(self, d, s, k):
            half = d if s == self.steps else None
            ref = self.piece(self.index(k), shift(self.p2, 1 - s if d == 0 else s - 1, self.n2), half)
            return remote(ref, ref, s2.at[self.phase, d], r2.at[self.phase, d, s - 1, k], self.dev[d])

        def forward(self, ref):
            return remote(ref, ref, ss.at[self.phase], sr.at[self.phase], sibling)

        def start(self):
            def step(k, _):
                self.direct(k).start()
                return 0

            lax.fori_loop(1, self.n1, step, 0)

        def own(self):
            def step(k, _):
                ref = self.piece(self.index(k), self.p2)

                @pl.when(k > 0)
                def _():
                    remote(ref, ref, s1.at[self.phase, k], r1.at[self.phase, k], sibling).wait_recv()

                for d in range(2):
                    self.copy(d, 1, k).start()
                self.forward(ref).start()
                return 0

            lax.fori_loop(0, self.n1, step, 0)

        def relay(self, s):
            def step(k, _):
                for d in range(2):
                    ref = self.at(d, s, k)
                    remote(ref, ref, s2.at[self.phase, d], r2.at[self.phase, d, s - 1, k],
                           self.dev[d]).wait_recv()
                    if s < self.steps:
                        self.copy(d, s + 1, k).start()
                    self.forward(ref).start()
                return 0

            lax.fori_loop(0, self.n1, step, 0)

        def sibling_done(self):
            ref = wbuf.at[self.js, 1 - self.cc]
            remote(ref, ref, ss.at[self.phase], sr.at[self.phase], sibling).wait_recv()

        def done(self):
            def step(k, _):
                self.direct(k).wait_send()
                return 0

            lax.fori_loop(1, self.n1, step, 0)
            if self.cc == 0:
                sent = wbuf.at[self.js, 0, 0 : X - 1, :, 0 : Y // 2]
            else:
                sent = wbuf.at[self.js, 1, :, 0 : ZL // 2, 0 : Y - 1]
            for d in range(2):
                remote(sent, sent, s2.at[self.phase, d], r2.at[self.phase, d, 0, 0],
                       self.dev[d]).wait_send()
            self.forward(wbuf.at[self.js, self.cc]).wait_send()

    def project(j, groups):
        chunk = depth // X

        def step(i, total):
            w = jnp.concatenate(
                [wbuf[j, cc, i].reshape(chunk, HD) for cc in groups], axis=1
            ) if len(groups) > 1 else wbuf[j, groups[0], i].reshape(chunk, HD)
            h = hbuf[:, pl.ds(pl.multiple_of(i * chunk, chunk), chunk)]
            return total + jnp.dot(h, w, preferred_element_type=jnp.float32)

        return lax.fori_loop(0, X, step, jnp.zeros((rows, HD * len(groups)), jnp.float32))

    def kv_copy(kind, way):
        if way == 0:
            return remote(kv.at[kind, ctx], kv.at[kind, ctx], kvs.at[kind, 0],
                          kvr.at[kind, ctx], ctx_right)
        if way == 1:
            return remote(kv.at[kind, ctx], kv.at[kind, ctx], kvs.at[kind, 1],
                          kvr.at[kind, ctx], ctx_left)
        b = before if kind == 0 else jnp.where(ctx == 0, 1, 0)
        dev = ctx_right if kind == 0 else ctx_left
        return remote(kv.at[kind, b], kv.at[kind, b], kvs.at[kind, 2], kvr.at[kind, b], dev)

    def kv_sends(kind, act):
        left = ctx == 0 if kind == 0 else ctx <= 1

        @pl.when(left)
        def _():
            act(kv_copy(kind, 1))

        @pl.when(ctx < ZH - 1)
        def _():
            act(kv_copy(kind, 0))

    def make(kind):
        if kind == 0:
            kv[0, ctx] = rotary(project(0, (0,)))
        else:
            kv[1, ctx] = project(0, (1,)).astype(jnp.bfloat16)
        kv_sends(kind, lambda c: c.start())

    def arrived(kind, b):
        remote(kv.at[kind, b], kv.at[kind, b], kvs.at[kind, 0], kvr.at[kind, b],
               ctx_right).wait_recv()

    def docs_arrived(b):
        remote(docs.at[b], docs.at[b], ds.at[0], dr.at[b], ctx_right).wait_recv()

    def relays():
        @pl.when((ctx == 1) | (ctx == 2))
        def _():
            docs_arrived(before)
            doc_relay.start()
            arrived(0, before)
            kv_copy(0, 2).start()

        @pl.when((ctx == 0) | (ctx == 3))
        def _():
            arrived(1, jnp.where(ctx == 0, 1, 0))
            kv_copy(1, 2).start()

    for cc in range(2):

        @pl.when(core == cc)
        def _():
            now, later_on = Gather(0, cc), Gather(1, cc)
            z_wait(0)
            now.start()
            now.own()
            for s in range(1, now.steps + 1):
                now.relay(s)
            z_wait(1)
            z_wait(2)
            later_on.start()
            hid_copy.wait()
            make(cc)
            now.sibling_done()
            make(1 - cc)
            later_on.own()
            for s in range(1, later_on.steps + 1):
                if s == later_on.steps:
                    relays()
                later_on.relay(s)
            later_on.sibling_done()
            now.done()
            later_on.done()

    for j in range(3):
        for k in range(1, 8):
            z_send(j, k).wait_send()

    for j in range(2):
        pair = project(1 + j, (0, 1))
        for i in range(2):
            qs[2 * j + i] = rotary(pair[:, i * HD : (i + 1) * HD])

    token = lax.broadcasted_iota(jnp.int32, (rows, 1), 0)
    zeros_here = jnp.sum(jnp.where(doc[...] == 0, 1.0, 0.0), axis=1, keepdims=True)
    doc_query = jnp.where(token.astype(jnp.float32) >= zeros_here, 1.0, 0.0)

    def scores(h, b):
        s = lax.dot_general(
            qs[h], kv[0, b], (((1,), (1,)), ((), ())), preferred_element_type=jnp.float32
        )
        return s * SCALE2 + bias[...]

    same = doc_query == doc[...].astype(jnp.float32)
    causal = lax.broadcasted_iota(jnp.int32, (rows, rows), 1) <= token
    bias[...] = jnp.where(same & causal, 0.0, -jnp.inf)

    def first(h, _):
        s = scores(h, ctx)
        top = jnp.max(s, axis=1, keepdims=True)
        p = jnp.exp2(s - top)
        m_s[h] = top
        l_s[h] = jnp.sum(p, axis=1, keepdims=True)
        acc[h] = jnp.dot(p.astype(jnp.bfloat16), kv[1, ctx], preferred_element_type=jnp.float32)
        return 0

    lax.fori_loop(0, HEADS, first, 0)

    def later(t, _):
        b = jnp.where(t == 0, ctx - 1, t - 1)

        @pl.when(jnp.logical_not(((ctx == 1) | (ctx == 2)) & (b == ctx - 1)))
        def _():
            docs_arrived(b)
            arrived(0, b)

        @pl.when(jnp.logical_not((ctx == 3) & (b == 0)))
        def _():
            arrived(1, b)

        bias[...] = jnp.where(doc_query == docs[b].astype(jnp.float32), 0.0, -jnp.inf)

        def update(h, _):
            s = scores(h, b)
            old = m_s[h]
            top = jnp.maximum(old, jnp.max(s, axis=1, keepdims=True))
            p = jnp.exp2(s - top)
            factor = jnp.exp2(old - top)
            m_s[h] = top
            l_s[h] = l_s[h] * factor + jnp.sum(p, axis=1, keepdims=True)
            acc[h] = acc[h] * factor + jnp.dot(
                p.astype(jnp.bfloat16), kv[1, b], preferred_element_type=jnp.float32
            )
            return 0

        lax.fori_loop(0, HEADS, update, 0)
        return 0

    lax.fori_loop(0, ctx, later, 0)

    for h in range(HEADS):
        out[:, h * HD : (h + 1) * HD] = (acc[h] / l_s[h]).astype(jnp.bfloat16)

    for kind in range(2):
        kv_sends(kind, lambda c: c.wait_send())

    @pl.when(ctx < ZH - 1)
    def _():
        doc_right.wait_send()

    @pl.when(ctx == 0)
    def _():
        doc_left.wait_send()

    @pl.when((ctx == 1) | (ctx == 2))
    def _():
        doc_relay.wait_send()
        kv_copy(0, 2).wait_send()

    @pl.when((ctx == 0) | (ctx == 3))
    def _():
        kv_copy(1, 2).wait_send()


def body(hidden_states, qkv_weight, doc_ids):
    rows, width = hidden_states.shape[1:]
    shard = qkv_weight.shape[0]
    dma = pltpu.SemaphoreType.DMA
    steps = max(X, Y) // 2
    result = pl.pallas_call(
        kernel,
        out_shape=jax.ShapeDtypeStruct((rows, HEADS * HD), jnp.bfloat16),
        in_specs=[
            pl.BlockSpec(memory_space=pl.ANY),
            pl.BlockSpec(memory_space=pl.ANY),
            pl.BlockSpec(memory_space=pltpu.VMEM),
        ],
        out_specs=pl.BlockSpec(memory_space=pltpu.VMEM),
        scratch_shapes=[
            pltpu.VMEM((3, 2, X, ZL, Y, 2 * shard, HD), jnp.bfloat16),
            pltpu.VMEM((rows, width), jnp.bfloat16),
            pltpu.VMEM((2, ZH, rows, HD), jnp.bfloat16),
            pltpu.VMEM((ZH, 1, rows), jnp.int32),
            pltpu.VMEM((HEADS, rows, HD), jnp.bfloat16),
            pltpu.VMEM((HEADS, rows, HD), jnp.float32),
            pltpu.VMEM((HEADS, rows, 1), jnp.float32),
            pltpu.VMEM((HEADS, rows, 1), jnp.float32),
            pltpu.VMEM((rows, rows), jnp.float32),
            pltpu.VMEM((rows, HD), jnp.float32),
            pltpu.VMEM((rows, HD), jnp.float32),
            dma((1,)),
            dma((3, 8)),
            dma((3, 8)),
            dma((2, Y)),
            dma((2, Y)),
            dma((2, 2)),
            dma((2, 2, steps, Y)),
            dma((2,)),
            dma((2,)),
            dma((2, 3)),
            dma((2, ZH)),
            dma((3,)),
            dma((ZH,)),
        ],
        compiler_params=pltpu.CompilerParams(
            collective_id=0, has_side_effects=True, vmem_limit_bytes=60 * 1024 * 1024
        ),
    )(hidden_states, qkv_weight, doc_ids)
    return result[None]


def solution(mesh):
    in_specs = (P("fsdp", "ctx", None), P("fsdp", None), P("fsdp", "ctx"))
    out_specs = P("fsdp", "ctx", None)
    return jax.shard_map(body, mesh=mesh, in_specs=in_specs, out_specs=out_specs, check_vma=False)
```

```python
import functools
import math

import jax
import jax.numpy as jnp
from jax import lax
from jax.experimental import pallas as pl
from jax.experimental.pallas import tpu as pltpu
from jax.sharding import PartitionSpec as P

MESH = pl.DeviceIdType.MESH
HEADS = 4
HD = 128
THETA = 1000000.0
X, ZL, Y, ZH = 4, 4, 8, 4
Z = ZL * ZH
SCALE2 = math.log2(math.e) / math.sqrt(HD)


def kernel(hid, w_in, doc, out, wbuf, hbuf, kv, docs, qs, acc, m_s, l_s, bias, cos_s, sin_s,
           loc_sem, zs, zr, s1, r1, s2, r2, ss, sr, kvs, kvr, ds, dr):
    rows = hid.shape[1]
    shard = w_in.shape[0]
    depth = X * ZL * Y * 2 * shard
    f = lax.axis_index("fsdp")
    ctx = lax.axis_index("ctx")
    core = lax.rem(f, 2)
    y = lax.rem(f // 2, Y)
    zl = lax.rem(f // (2 * Y), ZL)
    x = f // (2 * Y * ZL)
    z = ctx * ZL + zl

    def device(x_, z_, y_, core_):
        return {"fsdp": ((x_ * ZL + lax.rem(z_, ZL)) * Y + y_) * 2 + core_, "ctx": z_ // ZL}

    def shift(v, d, n):
        return lax.rem(v + d + n, n)

    z_peers = [shift(z, 1, Z), shift(z, -1, Z), shift(z, 2, Z)]
    sibling = device(x, z, y, 1 - core)
    x_right, x_left = device(shift(x, 1, X), z, y, core), device(shift(x, -1, X), z, y, core)
    y_right, y_left = device(x, z, shift(y, 1, Y), core), device(x, z, shift(y, -1, Y), core)
    ctx_right = {"fsdp": f, "ctx": shift(ctx, 1, ZH)}
    ctx_left = {"fsdp": f, "ctx": shift(ctx, -1, ZH)}

    def remote(src, dst, send, recv, dev):
        return pltpu.make_async_remote_copy(
            src_ref=src, dst_ref=dst, send_sem=send, recv_sem=recv, device_id=dev,
            device_id_type=MESH,
        )

    barrier = pltpu.get_barrier_semaphore()
    peers = [ctx_right, ctx_left, sibling]
    peers += [device(shift(x, d, X), z, y, core) for d in range(1, X)]
    peers += [device(x, z, shift(y, d, Y), core) for d in range(1, Y)]
    for z_ in z_peers + [shift(z, -2, Z)]:
        peers += [device(x, z_, y, 0), device(x, z_, y, 1)]
    hid_copy = pltpu.make_async_copy(hid.at[0], hbuf, loc_sem.at[0])
    hid_copy.start()
    for dev in peers:
        pl.semaphore_signal(barrier, inc=1, device_id=dev, device_id_type=MESH)
    pl.semaphore_wait(barrier, len(peers))

    def column(j, cc):
        start = (HEADS + cc) * HD if j == 0 else ((j - 1) * 2 + cc) * HD
        return pl.ds(pl.multiple_of(start, HD), HD)

    def z_slot(j, cc, zl_, core_):
        return wbuf.at[j, cc, x, zl_, y, pl.ds(pl.multiple_of(core_ * shard, shard), shard)]

    def z_send(j, k):
        cc = 1 - core if k % 2 else core
        if k < 2:
            dev = sibling
        else:
            dev = device(x, z_peers[k // 2 - 1], y, cc)
        return remote(
            w_in.at[:, column(j, cc)], z_slot(j, cc, zl, core), zs.at[j, k], zr.at[j, k], dev
        )

    def z_own(j):
        return pltpu.make_async_copy(
            w_in.at[:, column(j, core)], z_slot(j, core, zl, core), zr.at[j, 0]
        )

    def z_wait(j):
        z_own(j).wait()
        for k in range(1, 8):
            from_core = 1 - core if k % 2 else core
            from_zl = lax.rem(zl + (0, -1, 1, -2)[k // 2] + ZL, ZL)
            slot = z_slot(j, core, from_zl, from_core)
            remote(slot, slot, zs.at[j, k], zr.at[j, k], sibling).wait_recv()

    def z_start(j):
        for k in (7, 6, 5, 4, 3, 2, 1):
            z_send(j, k).start()
        z_own(j).start()

    z_start(0)

    doc_right = remote(doc, docs.at[ctx], ds.at[0], dr.at[ctx], ctx_right)
    doc_left = remote(doc, docs.at[ctx], ds.at[1], dr.at[ctx], ctx_left)
    before = jnp.maximum(ctx - 1, 0)
    doc_relay = remote(docs.at[before], docs.at[before], ds.at[2], dr.at[before], ctx_right)

    def aside():
        @pl.when(ctx < ZH - 1)
        def _():
            doc_right.start()

        @pl.when(ctx == 0)
        def _():
            doc_left.start()

        z_start(1)
        z_start(2)

        lane = lax.broadcasted_iota(jnp.int32, (1, HD), 1)
        half_lane = jnp.where(lane < HD // 2, lane, lane - HD // 2).astype(jnp.float32)
        frequency = jnp.exp(half_lane * (-2.0 * math.log(THETA) / HD))
        position = (ctx * rows + lax.broadcasted_iota(jnp.int32, (rows, 1), 0)).astype(jnp.float32)
        angles = position * frequency
        cos_s[...] = jnp.cos(angles)
        sin_s[...] = jnp.sin(angles) * jnp.where(lane < HD // 2, -1.0, 1.0)

    def rotary(v):
        return (v * cos_s[...] + pltpu.roll(v, HD // 2, 1) * sin_s[...]).astype(jnp.bfloat16)

    class Gather:
        def __init__(self, phase, cc):
            self.phase, self.cc = phase, cc
            self.js = slice(0, 1) if phase == 0 else slice(1, 3)
            self.n1, self.p1 = (Y, y) if cc == 0 else (X, x)
            self.n2, self.p2 = (X, x) if cc == 0 else (Y, y)
            self.dev = (x_right, x_left) if cc == 0 else (y_right, y_left)
            self.steps = self.n2 // 2

        def piece(self, i, q, half=None):
            zz = slice(None) if half is None else slice(half * (ZL // 2), (half + 1) * (ZL // 2))
            if self.cc == 0:
                return wbuf.at[self.js, 0, q, zz, i]
            return wbuf.at[self.js, 1, i, zz, q]

        def offset(self, k):
            return (k + 1) // 2 * (1 - 2 * lax.rem(k + 1, 2))

        def direct(self, k):
            ref = self.piece(self.p1, self.p2)
            to = lax.rem(self.p1 + self.offset(k) + self.n1, self.n1)
            dev = device(x, z, to, core) if self.cc == 0 else device(to, z, y, core)
            return remote(ref, ref, s1.at[self.phase, k], r1.at[self.phase, k], dev)

        def index(self, k):
            return lax.rem(self.p1 - self.offset(k) + self.n1, self.n1)

        def at(self, d, s, k):
            half = d if s == self.steps else None
            return self.piece(self.index(k), shift(self.p2, -s if d == 0 else s, self.n2), half)

        def copy(self, d, s, k):
            half = d if s == self.steps else None
            ref = self.piece(self.index(k), shift(self.p2, 1 - s if d == 0 else s - 1, self.n2), half)
            return remote(ref, ref, s2.at[self.phase, d], r2.at[self.phase, d, s - 1, k], self.dev[d])

        def forward(self, ref):
            return remote(ref, ref, ss.at[self.phase], sr.at[self.phase], sibling)

        def start(self):
            def step(k, _):
                self.direct(k).start()
                return 0

            lax.fori_loop(1, self.n1, step, 0)

        def own(self):
            def step(k, _):
                ref = self.piece(self.index(k), self.p2)

                @pl.when(k > 0)
                def _():
                    remote(ref, ref, s1.at[self.phase, k], r1.at[self.phase, k], sibling).wait_recv()

                for d in range(2):
                    self.copy(d, 1, k).start()
                self.forward(ref).start()
                return 0

            lax.fori_loop(0, self.n1, step, 0)

        def relay(self, s):
            def step(k, _):
                for d in range(2):
                    ref = self.at(d, s, k)
                    remote(ref, ref, s2.at[self.phase, d], r2.at[self.phase, d, s - 1, k],
                           self.dev[d]).wait_recv()
                    if s < self.steps:
                        self.copy(d, s + 1, k).start()
                    self.forward(ref).start()
                return 0

            lax.fori_loop(0, self.n1, step, 0)

        def sibling_done(self):
            ref = wbuf.at[self.js, 1 - self.cc]
            remote(ref, ref, ss.at[self.phase], sr.at[self.phase], sibling).wait_recv()

        def done(self):
            def step(k, _):
                self.direct(k).wait_send()
                return 0

            lax.fori_loop(1, self.n1, step, 0)
            if self.cc == 0:
                sent = wbuf.at[self.js, 0, 0 : X - 1, :, 0 : Y // 2]
            else:
                sent = wbuf.at[self.js, 1, :, 0 : ZL // 2, 0 : Y - 1]
            for d in range(2):
                remote(sent, sent, s2.at[self.phase, d], r2.at[self.phase, d, 0, 0],
                       self.dev[d]).wait_send()
            self.forward(wbuf.at[self.js, self.cc]).wait_send()

    def project(j, groups):
        chunk = depth // X

        def step(i, total):
            w = jnp.concatenate(
                [wbuf[j, cc, i].reshape(chunk, HD) for cc in groups], axis=1
            ) if len(groups) > 1 else wbuf[j, groups[0], i].reshape(chunk, HD)
            h = hbuf[:, pl.ds(pl.multiple_of(i * chunk, chunk), chunk)]
            return total + jnp.dot(h, w, preferred_element_type=jnp.float32)

        return lax.fori_loop(0, X, step, jnp.zeros((rows, HD * len(groups)), jnp.float32))

    one, two = core, 1 - core

    def kv_right(kind):
        return remote(kv.at[kind, ctx], kv.at[kind, ctx], kvs.at[kind, 0], kvr.at[kind, ctx],
                      ctx_right)

    def kv_left(kind):
        return remote(kv.at[kind, ctx], kv.at[kind, ctx], kvs.at[kind, 1], kvr.at[kind, ctx],
                      ctx_left)

    def kv_relay(kind, b, dev):
        return remote(kv.at[kind, b], kv.at[kind, b], kvs.at[kind, 2], kvr.at[kind, b], dev)

    def kv_half(i, dev):
        ref = kv.at[two, 0, i * (rows // 2) : (i + 1) * (rows // 2)]
        return remote(ref, ref, kvs.at[two, 2], kvr.at[two, i * ZH], dev)

    def kv_sends(first, act):
        kind = one if first else two

        @pl.when((ctx == 0) if first else (ctx <= 1))
        def _():
            act(kv_left(kind))

        @pl.when(ctx < ZH - 1)
        def _():
            act(kv_right(kind))

    def make(kind, first):
        if kind == 0:
            kv[0, ctx] = rotary(project(0, (0,)))
        else:
            kv[1, ctx] = project(0, (1,)).astype(jnp.bfloat16)
        kv_sends(first, lambda c: c.start())

    def arrived(kind, b):
        remote(kv.at[kind, b], kv.at[kind, b], kvs.at[kind, 0], kvr.at[kind, b],
               ctx_right).wait_recv()

    def docs_arrived(b):
        remote(docs.at[b], docs.at[b], ds.at[0], dr.at[b], ctx_right).wait_recv()

    def early_relays(act):
        @pl.when((ctx == 1) | (ctx == 2))
        def _():
            act(doc_relay)

        @pl.when(ctx == 2)
        def _():
            act(kv_relay(one, 1, ctx_right))

        @pl.when(ctx == 3)
        def _():
            act(kv_relay(one, 0, ctx_left))

        @pl.when(ctx == 0)
        def _():
            act(kv_relay(two, 1, ctx_left))

    def late_relays(act):
        @pl.when(ctx == 1)
        def _():
            act(kv_half(0, ctx_right))

        @pl.when(ctx == 3)
        def _():
            act(kv_half(1, ctx_left))

    def early_waits():
        @pl.when((ctx == 1) | (ctx == 2))
        def _():
            docs_arrived(before)

        @pl.when(ctx == 2)
        def _():
            arrived(one, 1)

        @pl.when(ctx == 3)
        def _():
            arrived(one, 0)

        @pl.when(ctx == 0)
        def _():
            arrived(two, 1)

    for cc in range(2):

        @pl.when(core == cc)
        def _():
            now, later_on = Gather(0, cc), Gather(1, cc)
            z_wait(0)
            now.start()
            aside()
            now.own()
            for s in range(1, now.steps + 1):
                now.relay(s)
            z_wait(1)
            z_wait(2)
            later_on.start()
            hid_copy.wait()
            make(cc, True)
            now.sibling_done()
            make(1 - cc, False)
            later_on.own()
            for s in range(1, later_on.steps + 1):
                if s == later_on.steps:
                    early_waits()
                    early_relays(lambda c: c.start())
                later_on.relay(s)
            later_on.sibling_done()
            now.done()
            later_on.done()

    for j in range(3):
        for k in range(1, 8):
            z_send(j, k).wait_send()

    for j in range(2):
        pair = project(1 + j, (0, 1))
        for i in range(2):
            qs[2 * j + i] = rotary(pair[:, i * HD : (i + 1) * HD])

    token = lax.broadcasted_iota(jnp.int32, (rows, 1), 0)
    zeros_here = jnp.sum(jnp.where(doc[...] == 0, 1.0, 0.0), axis=1, keepdims=True)
    doc_query = jnp.where(token.astype(jnp.float32) >= zeros_here, 1.0, 0.0)

    def scores(h, b):
        s = lax.dot_general(
            qs[h], kv[0, b], (((1,), (1,)), ((), ())), preferred_element_type=jnp.float32
        )
        return s * SCALE2 + bias[...]

    same = doc_query == doc[...].astype(jnp.float32)
    causal = lax.broadcasted_iota(jnp.int32, (rows, rows), 1) <= token
    bias[...] = jnp.where(same & causal, 0.0, -jnp.inf)

    def first(h, _):
        s = scores(h, ctx)
        top = jnp.max(s, axis=1, keepdims=True)
        p = jnp.exp2(s - top)
        m_s[h] = top
        l_s[h] = jnp.sum(p, axis=1, keepdims=True)
        acc[h] = jnp.dot(p.astype(jnp.bfloat16), kv[1, ctx], preferred_element_type=jnp.float32)
        return 0

    lax.fori_loop(0, HEADS, first, 0)

    @pl.when((ctx == 1) | (ctx == 3))
    def _():
        arrived(two, 0)

    late_relays(lambda c: c.start())

    def later(t, _):
        b = jnp.where(t == 0, ctx - 1, t - 1)

        @pl.when(jnp.logical_not(((ctx == 1) | (ctx == 2)) & (b == ctx - 1)))
        def _():
            docs_arrived(b)

        @pl.when(jnp.logical_not(((ctx == 2) & (b == 1)) | ((ctx == 3) & (b == 0))))
        def _():
            arrived(one, b)

        @pl.when(b > 0)
        def _():
            arrived(two, b)

        @pl.when((ctx == 2) & (b == 0))
        def _():
            kv_half(0, ctx_right).wait_recv()
            kv_half(1, ctx_right).wait_recv()

        bias[...] = jnp.where(doc_query == docs[b].astype(jnp.float32), 0.0, -jnp.inf)

        def update(h, _):
            s = scores(h, b)
            old = m_s[h]
            top = jnp.maximum(old, jnp.max(s, axis=1, keepdims=True))
            p = jnp.exp2(s - top)
            factor = jnp.exp2(old - top)
            m_s[h] = top
            l_s[h] = l_s[h] * factor + jnp.sum(p, axis=1, keepdims=True)
            acc[h] = acc[h] * factor + jnp.dot(
                p.astype(jnp.bfloat16), kv[1, b], preferred_element_type=jnp.float32
            )
            return 0

        lax.fori_loop(0, HEADS, update, 0)
        return 0

    lax.fori_loop(0, ctx, later, 0)

    for h in range(HEADS):
        out[:, h * HD : (h + 1) * HD] = (acc[h] / l_s[h]).astype(jnp.bfloat16)

    for first_sent in (True, False):
        kv_sends(first_sent, lambda c: c.wait_send())
    early_relays(lambda c: c.wait_send())
    late_relays(lambda c: c.wait_send())

    @pl.when(ctx < ZH - 1)
    def _():
        doc_right.wait_send()

    @pl.when(ctx == 0)
    def _():
        doc_left.wait_send()


def body(hidden_states, qkv_weight, doc_ids):
    rows, width = hidden_states.shape[1:]
    shard = qkv_weight.shape[0]
    dma = pltpu.SemaphoreType.DMA
    steps = max(X, Y) // 2
    result = pl.pallas_call(
        kernel,
        out_shape=jax.ShapeDtypeStruct((rows, HEADS * HD), jnp.bfloat16),
        in_specs=[
            pl.BlockSpec(memory_space=pl.ANY),
            pl.BlockSpec(memory_space=pl.ANY),
            pl.BlockSpec(memory_space=pltpu.VMEM),
        ],
        out_specs=pl.BlockSpec(memory_space=pltpu.VMEM),
        scratch_shapes=[
            pltpu.VMEM((3, 2, X, ZL, Y, 2 * shard, HD), jnp.bfloat16),
            pltpu.VMEM((rows, width), jnp.bfloat16),
            pltpu.VMEM((2, ZH, rows, HD), jnp.bfloat16),
            pltpu.VMEM((ZH, 1, rows), jnp.int32),
            pltpu.VMEM((HEADS, rows, HD), jnp.bfloat16),
            pltpu.VMEM((HEADS, rows, HD), jnp.float32),
            pltpu.VMEM((HEADS, rows, 1), jnp.float32),
            pltpu.VMEM((HEADS, rows, 1), jnp.float32),
            pltpu.VMEM((rows, rows), jnp.float32),
            pltpu.VMEM((rows, HD), jnp.float32),
            pltpu.VMEM((rows, HD), jnp.float32),
            dma((1,)),
            dma((3, 8)),
            dma((3, 8)),
            dma((2, Y)),
            dma((2, Y)),
            dma((2, 2)),
            dma((2, 2, steps, Y)),
            dma((2,)),
            dma((2,)),
            dma((2, 3)),
            dma((2, ZH + 1)),
            dma((3,)),
            dma((ZH,)),
        ],
        compiler_params=pltpu.CompilerParams(
            collective_id=0, has_side_effects=True, vmem_limit_bytes=60 * 1024 * 1024
        ),
    )(hidden_states, qkv_weight, doc_ids)
    return result[None]


def solution(mesh):
    in_specs = (P("fsdp", "ctx", None), P("fsdp", None), P("fsdp", "ctx"))
    out_specs = P("fsdp", "ctx", None)
    return jax.shard_map(body, mesh=mesh, in_specs=in_specs, out_specs=out_specs, check_vma=False)
```

```python
import functools
import math

import jax
import jax.numpy as jnp
from jax import lax
from jax.experimental import pallas as pl
from jax.experimental.pallas import tpu as pltpu
from jax.sharding import PartitionSpec as P

MESH = pl.DeviceIdType.MESH
HEADS = 4
HD = 128
THETA = 1000000.0
X, ZL, Y, ZH = 4, 4, 8, 4
Z = ZL * ZH
SCALE2 = math.log2(math.e) / math.sqrt(HD)


def kernel(hid, w_in, doc, out, wbuf, hbuf, kv, docs, qs, acc, m_s, l_s, bias, cos_s, sin_s,
           loc_sem, zs, zr, s1, r1, s2, r2, ss, sr, kvs, kvr, ds, dr):
    rows = hid.shape[1]
    shard = w_in.shape[0]
    depth = X * ZL * Y * 2 * shard
    f = lax.axis_index("fsdp")
    ctx = lax.axis_index("ctx")
    core = lax.rem(f, 2)
    y = lax.rem(f // 2, Y)
    zl = lax.rem(f // (2 * Y), ZL)
    x = f // (2 * Y * ZL)
    z = ctx * ZL + zl

    def device(x_, z_, y_, core_):
        return {"fsdp": ((x_ * ZL + lax.rem(z_, ZL)) * Y + y_) * 2 + core_, "ctx": z_ // ZL}

    def shift(v, d, n):
        return lax.rem(v + d + n, n)

    z_peers = [shift(z, 1, Z), shift(z, -1, Z), shift(z, 2, Z)]
    sibling = device(x, z, y, 1 - core)
    x_right, x_left = device(shift(x, 1, X), z, y, core), device(shift(x, -1, X), z, y, core)
    y_right, y_left = device(x, z, shift(y, 1, Y), core), device(x, z, shift(y, -1, Y), core)
    ctx_right = {"fsdp": f, "ctx": shift(ctx, 1, ZH)}
    ctx_left = {"fsdp": f, "ctx": shift(ctx, -1, ZH)}

    def remote(src, dst, send, recv, dev):
        return pltpu.make_async_remote_copy(
            src_ref=src, dst_ref=dst, send_sem=send, recv_sem=recv, device_id=dev,
            device_id_type=MESH,
        )

    barrier = pltpu.get_barrier_semaphore()
    peers = [ctx_right, ctx_left, sibling]
    peers += [device(shift(x, d, X), z, y, core) for d in range(1, X)]
    peers += [device(x, z, shift(y, d, Y), core) for d in range(1, Y)]
    for z_ in z_peers + [shift(z, -2, Z)]:
        peers += [device(x, z_, y, 0), device(x, z_, y, 1)]
    hid_copy = pltpu.make_async_copy(hid.at[0], hbuf, loc_sem.at[0])
    hid_copy.start()
    for dev in peers:
        pl.semaphore_signal(barrier, inc=1, device_id=dev, device_id_type=MESH)
    pl.semaphore_wait(barrier, len(peers))

    def column(j, cc):
        start = (HEADS + cc) * HD if j == 0 else ((j - 1) * 2 + cc) * HD
        return pl.ds(pl.multiple_of(start, HD), HD)

    def z_slot(j, cc, zl_, core_):
        return wbuf.at[j, cc, x, zl_, y, pl.ds(pl.multiple_of(core_ * shard, shard), shard)]

    def z_send(j, k):
        cc = 1 - core if k % 2 else core
        if k < 2:
            dev = sibling
        else:
            dev = device(x, z_peers[k // 2 - 1], y, cc)
        return remote(
            w_in.at[:, column(j, cc)], z_slot(j, cc, zl, core), zs.at[j, k], zr.at[j, k], dev
        )

    def z_own(j):
        return pltpu.make_async_copy(
            w_in.at[:, column(j, core)], z_slot(j, core, zl, core), zr.at[j, 0]
        )

    def z_wait(j):
        z_own(j).wait()
        for k in range(1, 8):
            from_core = 1 - core if k % 2 else core
            from_zl = lax.rem(zl + (0, -1, 1, -2)[k // 2] + ZL, ZL)
            slot = z_slot(j, core, from_zl, from_core)
            remote(slot, slot, zs.at[j, k], zr.at[j, k], sibling).wait_recv()

    def z_start(j):
        for k in (7, 6, 5, 4, 3, 2, 1):
            z_send(j, k).start()
        z_own(j).start()

    z_start(0)

    doc_right = remote(doc, docs.at[ctx], ds.at[0], dr.at[ctx], ctx_right)
    doc_left = remote(doc, docs.at[ctx], ds.at[1], dr.at[ctx], ctx_left)
    before = jnp.maximum(ctx - 1, 0)
    doc_relay = remote(docs.at[before], docs.at[before], ds.at[2], dr.at[before], ctx_right)

    def aside():
        @pl.when(ctx < ZH - 1)
        def _():
            doc_right.start()

        @pl.when(ctx == 0)
        def _():
            doc_left.start()

        z_start(1)
        z_start(2)

        lane = lax.broadcasted_iota(jnp.int32, (1, HD), 1)
        half_lane = jnp.where(lane < HD // 2, lane, lane - HD // 2).astype(jnp.float32)
        frequency = jnp.exp(half_lane * (-2.0 * math.log(THETA) / HD))
        position = (ctx * rows + lax.broadcasted_iota(jnp.int32, (rows, 1), 0)).astype(jnp.float32)
        angles = position * frequency
        cos_s[...] = jnp.cos(angles)
        sin_s[...] = jnp.sin(angles) * jnp.where(lane < HD // 2, -1.0, 1.0)

    def rotary(v):
        return (v * cos_s[...] + pltpu.roll(v, HD // 2, 1) * sin_s[...]).astype(jnp.bfloat16)

    class Gather:
        def __init__(self, phase, cc):
            self.phase, self.cc = phase, cc
            self.js = slice(0, 1) if phase == 0 else slice(1, 3)
            self.n1, self.p1 = (Y, y) if cc == 0 else (X, x)
            self.n2, self.p2 = (X, x) if cc == 0 else (Y, y)
            self.dev = (x_right, x_left) if cc == 0 else (y_right, y_left)
            self.steps = self.n2 // 2

        def piece(self, i, q, half=None):
            zz = slice(None) if half is None else slice(half * (ZL // 2), (half + 1) * (ZL // 2))
            if self.cc == 0:
                return wbuf.at[self.js, 0, q, zz, i]
            return wbuf.at[self.js, 1, i, zz, q]

        def offset(self, k):
            return (k + 1) // 2 * (1 - 2 * lax.rem(k + 1, 2))

        def direct(self, k):
            ref = self.piece(self.p1, self.p2)
            to = lax.rem(self.p1 + self.offset(k) + self.n1, self.n1)
            dev = device(x, z, to, core) if self.cc == 0 else device(to, z, y, core)
            return remote(ref, ref, s1.at[self.phase, k], r1.at[self.phase, k], dev)

        def index(self, k):
            return lax.rem(self.p1 - self.offset(k) + self.n1, self.n1)

        def at(self, d, s, k):
            half = d if s == self.steps else None
            return self.piece(self.index(k), shift(self.p2, -s if d == 0 else s, self.n2), half)

        def copy(self, d, s, k):
            half = d if s == self.steps else None
            ref = self.piece(self.index(k), shift(self.p2, 1 - s if d == 0 else s - 1, self.n2), half)
            return remote(ref, ref, s2.at[self.phase, d], r2.at[self.phase, d, s - 1, k], self.dev[d])

        def forward(self, ref):
            return remote(ref, ref, ss.at[self.phase], sr.at[self.phase], sibling)

        def start(self):
            def step(k, _):
                self.direct(k).start()
                return 0

            lax.fori_loop(1, self.n1, step, 0)

        def own(self):
            def step(k, _):
                ref = self.piece(self.index(k), self.p2)

                @pl.when(k > 0)
                def _():
                    remote(ref, ref, s1.at[self.phase, k], r1.at[self.phase, k], sibling).wait_recv()

                for d in range(2):
                    self.copy(d, 1, k).start()
                self.forward(ref).start()
                return 0

            lax.fori_loop(0, self.n1, step, 0)

        def relay(self, s):
            def step(k, _):
                for d in range(2):
                    ref = self.at(d, s, k)
                    remote(ref, ref, s2.at[self.phase, d], r2.at[self.phase, d, s - 1, k],
                           self.dev[d]).wait_recv()
                    if s < self.steps:
                        self.copy(d, s + 1, k).start()
                    self.forward(ref).start()
                return 0

            lax.fori_loop(0, self.n1, step, 0)

        def sibling_done(self):
            ref = wbuf.at[self.js, 1 - self.cc]
            remote(ref, ref, ss.at[self.phase], sr.at[self.phase], sibling).wait_recv()

        def done(self):
            def step(k, _):
                self.direct(k).wait_send()
                return 0

            lax.fori_loop(1, self.n1, step, 0)
            if self.cc == 0:
                sent = wbuf.at[self.js, 0, 0 : X - 1, :, 0 : Y // 2]
            else:
                sent = wbuf.at[self.js, 1, :, 0 : ZL // 2, 0 : Y - 1]
            for d in range(2):
                remote(sent, sent, s2.at[self.phase, d], r2.at[self.phase, d, 0, 0],
                       self.dev[d]).wait_send()
            self.forward(wbuf.at[self.js, self.cc]).wait_send()

    def project(j, groups):
        chunk = depth // X

        def step(i, total):
            w = jnp.concatenate(
                [wbuf[j, cc, i].reshape(chunk, HD) for cc in groups], axis=1
            ) if len(groups) > 1 else wbuf[j, groups[0], i].reshape(chunk, HD)
            h = hbuf[:, pl.ds(pl.multiple_of(i * chunk, chunk), chunk)]
            return total + jnp.dot(h, w, preferred_element_type=jnp.float32)

        return lax.fori_loop(0, X, step, jnp.zeros((rows, HD * len(groups)), jnp.float32))

    one, two = core, 1 - core

    def kv_right(kind):
        return remote(kv.at[kind, ctx], kv.at[kind, ctx], kvs.at[kind, 0], kvr.at[kind, ctx],
                      ctx_right)

    def kv_left(kind):
        return remote(kv.at[kind, ctx], kv.at[kind, ctx], kvs.at[kind, 1], kvr.at[kind, ctx],
                      ctx_left)

    def kv_relay(kind, b, dev):
        return remote(kv.at[kind, b], kv.at[kind, b], kvs.at[kind, 2], kvr.at[kind, b], dev)

    def kv_half(i, dev):
        ref = kv.at[two, 0, i * (rows // 2) : (i + 1) * (rows // 2)]
        return remote(ref, ref, kvs.at[two, 2], kvr.at[two, i * ZH], dev)

    def kv_sends(first, act):
        kind = one if first else two

        @pl.when((ctx == 0) if first else (ctx <= 1))
        def _():
            act(kv_left(kind))

        @pl.when(ctx < ZH - 1)
        def _():
            act(kv_right(kind))

    def make(kind, first):
        if kind == 0:
            kv[0, ctx] = rotary(project(0, (0,)))
        else:
            kv[1, ctx] = project(0, (1,)).astype(jnp.bfloat16)
        kv_sends(first, lambda c: c.start())

    def arrived(kind, b):
        remote(kv.at[kind, b], kv.at[kind, b], kvs.at[kind, 0], kvr.at[kind, b],
               ctx_right).wait_recv()

    def docs_arrived(b):
        remote(docs.at[b], docs.at[b], ds.at[0], dr.at[b], ctx_right).wait_recv()

    def early_relays(act):
        @pl.when((ctx == 1) | (ctx == 2))
        def _():
            act(doc_relay)

        @pl.when(ctx == 2)
        def _():
            act(kv_relay(one, 1, ctx_right))

        @pl.when(ctx == 3)
        def _():
            act(kv_relay(one, 0, ctx_left))

        @pl.when(ctx == 0)
        def _():
            act(kv_relay(two, 1, ctx_left))

    def late_relays(act):
        @pl.when(ctx == 1)
        def _():
            act(kv_half(0, ctx_right))

        @pl.when(ctx == 3)
        def _():
            act(kv_half(1, ctx_left))

    def early_waits():
        @pl.when((ctx == 1) | (ctx == 2))
        def _():
            docs_arrived(before)

        @pl.when(ctx == 2)
        def _():
            arrived(one, 1)

        @pl.when(ctx == 3)
        def _():
            arrived(one, 0)

        @pl.when(ctx == 0)
        def _():
            arrived(two, 1)

    for cc in range(2):

        @pl.when(core == cc)
        def _():
            now, later_on = Gather(0, cc), Gather(1, cc)
            z_wait(0)
            now.start()
            aside()
            now.own()
            for s in range(1, now.steps + 1):
                now.relay(s)
            z_wait(1)
            z_wait(2)
            later_on.start()
            hid_copy.wait()
            make(cc, True)
            now.sibling_done()
            make(1 - cc, False)
            later_on.own()
            for s in range(1, later_on.steps + 1):
                if s == later_on.steps:
                    early_waits()
                    early_relays(lambda c: c.start())
                later_on.relay(s)
            later_on.sibling_done()
            now.done()
            later_on.done()

    for j in range(3):
        for k in range(1, 8):
            z_send(j, k).wait_send()

    for j in range(2):
        pair = project(1 + j, (0, 1))
        for i in range(2):
            qs[2 * j + i] = rotary(pair[:, i * HD : (i + 1) * HD])

    token = lax.broadcasted_iota(jnp.int32, (rows, 1), 0)
    zeros_here = jnp.sum(jnp.where(doc[...] == 0, 1.0, 0.0), axis=1, keepdims=True)
    doc_query = jnp.where(token.astype(jnp.float32) >= zeros_here, 1.0, 0.0)

    def scores(h, b):
        s = lax.dot_general(
            qs[h], kv[0, b], (((1,), (1,)), ((), ())), preferred_element_type=jnp.float32
        )
        return s * SCALE2 + bias[...]

    same = doc_query == doc[...].astype(jnp.float32)
    causal = lax.broadcasted_iota(jnp.int32, (rows, rows), 1) <= token
    bias[...] = jnp.where(same & causal, 0.0, -jnp.inf)

    def first(h, _):
        s = scores(h, ctx)
        top = jnp.max(s, axis=1, keepdims=True)
        p = jnp.exp2(s - top)
        m_s[h] = top
        l_s[h] = jnp.sum(p, axis=1, keepdims=True)
        acc[h] = jnp.dot(p.astype(jnp.bfloat16), kv[1, ctx], preferred_element_type=jnp.float32)
        return 0

    lax.fori_loop(0, HEADS, first, 0)

    @pl.when((ctx == 1) | (ctx == 3))
    def _():
        arrived(two, 0)

    late_relays(lambda c: c.start())

    def later(t, _):
        b = jnp.where(t == 0, ctx - 1, t - 1)

        @pl.when(jnp.logical_not(((ctx == 1) | (ctx == 2)) & (b == ctx - 1)))
        def _():
            docs_arrived(b)

        @pl.when(jnp.logical_not(((ctx == 2) & (b == 1)) | ((ctx == 3) & (b == 0))))
        def _():
            arrived(one, b)

        @pl.when(b > 0)
        def _():
            arrived(two, b)

        @pl.when((ctx == 2) & (b == 0))
        def _():
            kv_half(0, ctx_right).wait_recv()
            kv_half(1, ctx_right).wait_recv()

        bias[...] = jnp.where(doc_query == docs[b].astype(jnp.float32), 0.0, -jnp.inf)

        def update(h, _):
            s = scores(h, b)
            old = m_s[h]
            top = jnp.maximum(old, jnp.max(s, axis=1, keepdims=True))
            p = jnp.exp2(s - top)
            factor = jnp.exp2(old - top)
            m_s[h] = top
            l_s[h] = l_s[h] * factor + jnp.sum(p, axis=1, keepdims=True)
            acc[h] = acc[h] * factor + jnp.dot(
                p.astype(jnp.bfloat16), kv[1, b], preferred_element_type=jnp.float32
            )
            return 0

        lax.fori_loop(0, HEADS, update, 0)
        return 0

    lax.fori_loop(0, ctx, later, 0)

    for h in range(HEADS):
        out[:, h * HD : (h + 1) * HD] = (acc[h] / l_s[h]).astype(jnp.bfloat16)

    for first_sent in (True, False):
        kv_sends(first_sent, lambda c: c.wait_send())
    early_relays(lambda c: c.wait_send())
    late_relays(lambda c: c.wait_send())

    @pl.when(ctx < ZH - 1)
    def _():
        doc_right.wait_send()

    @pl.when(ctx == 0)
    def _():
        doc_left.wait_send()


def body(hidden_states, qkv_weight, doc_ids):
    rows, width = hidden_states.shape[1:]
    shard = qkv_weight.shape[0]
    dma = pltpu.SemaphoreType.DMA
    steps = max(X, Y) // 2
    result = pl.pallas_call(
        kernel,
        out_shape=jax.ShapeDtypeStruct((rows, HEADS * HD), jnp.bfloat16),
        in_specs=[
            pl.BlockSpec(memory_space=pltpu.HBM),
            pl.BlockSpec(memory_space=pltpu.HBM),
            pl.BlockSpec(memory_space=pltpu.VMEM),
        ],
        out_specs=pl.BlockSpec(memory_space=pltpu.VMEM),
        scratch_shapes=[
            pltpu.VMEM((3, 2, X, ZL, Y, 2 * shard, HD), jnp.bfloat16),
            pltpu.VMEM((rows, width), jnp.bfloat16),
            pltpu.VMEM((2, ZH, rows, HD), jnp.bfloat16),
            pltpu.VMEM((ZH, 1, rows), jnp.int32),
            pltpu.VMEM((HEADS, rows, HD), jnp.bfloat16),
            pltpu.VMEM((HEADS, rows, HD), jnp.float32),
            pltpu.VMEM((HEADS, rows, 1), jnp.float32),
            pltpu.VMEM((HEADS, rows, 1), jnp.float32),
            pltpu.VMEM((rows, rows), jnp.float32),
            pltpu.VMEM((rows, HD), jnp.float32),
            pltpu.VMEM((rows, HD), jnp.float32),
            dma((1,)),
            dma((3, 8)),
            dma((3, 8)),
            dma((2, Y)),
            dma((2, Y)),
            dma((2, 2)),
            dma((2, 2, steps, Y)),
            dma((2,)),
            dma((2,)),
            dma((2, 3)),
            dma((2, ZH + 1)),
            dma((3,)),
            dma((ZH,)),
        ],
        compiler_params=pltpu.CompilerParams(
            collective_id=0, has_side_effects=True, vmem_limit_bytes=24 * 1024 * 1024
        ),
    )(pltpu.with_memory_space_constraint(hidden_states, pltpu.HBM), pltpu.with_memory_space_constraint(qkv_weight, pltpu.HBM), doc_ids)
    return result[None]


def solution(mesh):
    in_specs = (P("fsdp", "ctx", None), P("fsdp", None), P("fsdp", "ctx"))
    out_specs = P("fsdp", "ctx", None)
    return jax.shard_map(body, mesh=mesh, in_specs=in_specs, out_specs=out_specs, check_vma=False)
```
